32 devices in a mesh: blk: 4 (over y, x), grp: 8 (over z, core).
Axes of the slice: x: 2, y: 2, z: 4, core: 2. Of those that a mesh axis runs over, the one named last changes fastest.
Arguments:
- frames: bfloat16 [4096, 8, 2048], P(('blk', 'grp')), may hold values from -6 to 6
- counts: int32 [4096], P(('blk', 'grp')), may hold values from 1 to 8
- positives: int32 [4096], P(('blk', 'grp')), may hold values from 0 to 4095, as said below
- w_first: bfloat16 [2048, 4096], P(None, 'grp'), may hold values from -0.125 to 0.125
- w_second: bfloat16 [4096, 256], P('grp'), may hold values from -0.09375 to 0.09375
Outputs:
- batch_loss: float32 [], replicated
- grad_first: float32 [2048, 4096], P(None, 'grp')
- grad_second: float32 [4096, 256], P('grp')
The draws below stay inside these ranges and needn't reach their ends.
Inputs may be any that keep to these rules, and one draw needn't show every extreme that they name: positives[positives[i]] = i and positives[i] != i for every clip i.
All inputs are finite; a program needn't handle non-finite values.
Results may differ from the reference program's by a relative error of at most 0.005.
The reference program's roundings to bfloat16 on the way count: a program that leaves them out, or rounds other values in their place, can miss the bound.
Values may be sent and summed in bfloat16 or wider, within the bound.
A program may use at most 128 MiB of HBM per device.

```python
import jax
import jax.numpy as jnp
from jax import lax

C = 2048
H = 4096
E = 256
FRAMES = 8
GROUP_CLIPS = 1024
SEGMENT_COUNT = 4096


def draw_positives(key, part):
    order = jax.random.permutation(jax.random.fold_in(key, 17), SEGMENT_COUNT).astype(jnp.int32)
    first_half = order[0::2]
    second_half = order[1::2]
    paired = jnp.zeros((SEGMENT_COUNT,), jnp.int32).at[first_half].set(second_half).at[second_half].set(first_half)
    return paired.astype(jnp.int32)


def plant(drawn, key, low, high):
    place = [jax.random.randint(jax.random.fold_in(key, axis), (), 0, length) for axis, length in enumerate(drawn.shape)]
    main_axis = drawn.shape.index(max(drawn.shape))
    next_to = place[:main_axis] + [(place[main_axis] + 1) % drawn.shape[main_axis]] + place[main_axis + 1:]
    return drawn.at[tuple(place)].set(low).at[tuple(next_to)].set(high)


def levels(key, dims, shards, smallest, top_value):
    def one(position, parts):
        draws = jax.random.uniform(jax.random.fold_in(jax.random.fold_in(key, 6), position), (parts,), jnp.float32, smallest / len(shards), top_value / len(shards))
        return jnp.repeat(jnp.exp(draws), dims[position] // parts).reshape((-1,) + (1,) * (len(dims) - position - 1))

    level = one(*shards[0])
    for cut in shards[1:]:
        level = level * one(*cut)
    return level


def centred(key, dims, scale, reach, shards=(), kind=jnp.bfloat16):
    level = levels(key, dims, shards, -0.22, 0.18) if shards else 1.0
    values = jax.random.normal(key, dims, jnp.float32) * scale * level
    return jnp.minimum(jnp.maximum(values, -reach), reach).astype(kind)


def setup_inputs(seed: int = 0) -> dict:
    splits = jax.random.split(jax.random.key(seed), 6)
    return {
        "frames": centred(splits[0], (SEGMENT_COUNT, FRAMES, C), 1.0, 6.0, ((0, 32),)),
        "counts": plant(jax.random.randint(splits[1], (SEGMENT_COUNT,), 1, FRAMES + 1), jax.random.fold_in(splits[1], 1), 1, FRAMES).astype(jnp.int32),
        "positives": draw_positives(jax.random.fold_in(splits[5], 71), 0),
        "w_first": centred(splits[3], (C, H), C ** -0.5, 0.125, ((1, 8),)),
        "w_second": centred(splits[4], (H, E), H ** -0.5, 0.09375, ((0, 8),)),
    }


logit_sharpness_divisor = 0.05
score_top = 20.0

def reference(frames, counts, positives, w_first, w_second):
    frame_mask = (jnp.arange(FRAMES, dtype=jnp.int32)[None, :] < counts[:, None]).astype(jnp.float32)
    summed = jnp.einsum('rf,rfc->rc', frame_mask, frames.astype(jnp.float32))
    pooled = (summed / counts[:, None].astype(jnp.float32)).astype(jnp.bfloat16)
    preact = jnp.dot(pooled, w_first, preferred_element_type=jnp.float32)
    hidden = jax.nn.gelu(preact).astype(jnp.bfloat16)
    raw_keys = jnp.dot(hidden, w_second, preferred_element_type=jnp.float32)
    key_length = jnp.sqrt(lax.optimization_barrier(jnp.sum(raw_keys * raw_keys, axis=1, keepdims=True)) + 1e-06)
    unit_keys = raw_keys / key_length
    lower_match_vectors = unit_keys.astype(jnp.bfloat16)
    block_rows = GROUP_CLIPS
    block_count = SEGMENT_COUNT // block_rows
    all_ids = jnp.arange(SEGMENT_COUNT, dtype=jnp.int32)

    def block_scores(index):
        offset = (index * block_rows).astype(jnp.int32)
        lower_entry_span = lax.dynamic_slice_in_dim(lower_match_vectors, offset, block_rows, 0)
        cosine_logit_matrix = lax.dot_general(lower_entry_span, lower_match_vectors, (((1,), (1,)), ((), ())), preferred_element_type=jnp.float32) / logit_sharpness_divisor
        row_ids = offset + jnp.arange(block_rows, dtype=jnp.int32)
        partner = lax.dynamic_slice_in_dim(positives, offset, block_rows, 0)
        self_mask = all_ids[None, :] == row_ids[:, None]
        pair_mask = all_ids[None, :] == partner[:, None]
        return (lower_entry_span, cosine_logit_matrix, self_mask, pair_mask)

    def first_pass(index):
        lower_entry_span, cosine_logit_matrix, self_mask, pair_mask = block_scores(index)
        exp_terms = jnp.where(self_mask, 0.0, jnp.exp(cosine_logit_matrix - score_top))
        log_norm = jnp.log(lax.optimization_barrier(jnp.sum(exp_terms, axis=1))) + score_top
        pos_score = lax.optimization_barrier(jnp.sum(jnp.where(pair_mask, cosine_logit_matrix, 0.0), axis=1))
        return (log_norm, pos_score)
    log_norm, pos_score = lax.map(first_pass, jnp.arange(block_count, dtype=jnp.int32))
    log_norm = log_norm.reshape(SEGMENT_COUNT)
    pos_score = pos_score.reshape(SEGMENT_COUNT)
    batch_loss = jnp.sum(log_norm - pos_score) / SEGMENT_COUNT

    def second_pass(carry, index):
        lower_entry_span, cosine_logit_matrix, self_mask, pair_mask = block_scores(index)
        offset = (index * block_rows).astype(jnp.int32)
        row_norm = lax.dynamic_slice_in_dim(log_norm, offset, block_rows, 0)
        probs = jnp.where(self_mask, 0.0, jnp.exp(cosine_logit_matrix - row_norm[:, None]))
        weights = (probs - pair_mask.astype(jnp.float32)).astype(jnp.bfloat16)
        source_share = jnp.dot(weights, lower_match_vectors, preferred_element_type=jnp.float32)
        carry = carry + lax.dot_general(weights, lower_entry_span, (((0,), (0,)), ((), ())), preferred_element_type=jnp.float32)
        return (carry, source_share)
    target_share, source_share = lax.scan(second_pass, jnp.zeros((SEGMENT_COUNT, E), jnp.float32), jnp.arange(block_count, dtype=jnp.int32))
    source_share = source_share.reshape(SEGMENT_COUNT, E)
    sphere_projected_derivative = (source_share + target_share) / (SEGMENT_COUNT * logit_sharpness_divisor)
    raw_grad = ((sphere_projected_derivative - unit_keys * lax.optimization_barrier(jnp.sum(unit_keys * sphere_projected_derivative, axis=1, keepdims=True))) / key_length).astype(jnp.bfloat16)
    grad_second = lax.dot_general(hidden, raw_grad, (((0,), (0,)), ((), ())), preferred_element_type=jnp.float32)
    hidden_grad = lax.dot_general(raw_grad, w_second, (((1,), (1,)), ((), ())), preferred_element_type=jnp.float32)
    unused, backward = jax.vjp(jax.nn.gelu, preact)
    preact_grad = backward(hidden_grad)[0].astype(jnp.bfloat16)
    grad_first = lax.dot_general(pooled, preact_grad, (((0,), (0,)), ((), ())), preferred_element_type=jnp.float32)
    return (batch_loss, grad_first, grad_second)
```

```python
import functools

import jax
import jax.numpy as jnp
from jax import lax
from jax.experimental import pallas as pl
from jax.experimental.pallas import tpu as pltpu
from jax.sharding import PartitionSpec as P

sharpness = 20.0
score_top = 20.0
MESH = pl.DeviceIdType.MESH
F32 = jnp.float32
BF16 = jnp.bfloat16


def aligned(start, step):
    return pl.multiple_of(start, step)


def greet(partners):
    barrier = pltpu.get_barrier_semaphore()
    for device in partners:
        pl.semaphore_signal(barrier, inc=1, device_id=device, device_id_type=MESH)
    pl.semaphore_wait(barrier, len(partners))


def remote(src, dst, send_sem, recv_sem, device):
    return pltpu.make_async_remote_copy(
        src_ref=src,
        dst_ref=dst,
        send_sem=send_sem,
        recv_sem=recv_sem,
        device_id=device,
        device_id_type=MESH,
    )


def head_kernel(
    n, pooled_ref, first_ref, second_ref, all_ref, preact_ref, hidden_ref, partial_ref,
    ring_send, ring_recv, pair_send, pair_recv,
):
    rows = pooled_ref.shape[0]
    half = rows // 2
    steps = n // 2
    g = lax.axis_index("grp")
    z, c = g // 2, g % 2
    pair = {"grp": z * 2 + 1 - c}
    right = {"grp": ((z + 1) % n) * 2 + c}
    left = {"grp": ((z + n - 1) % n) * 2 + c}
    greet([pair, right, left])

    def block(chip, core, start=0, size=rows):
        return all_ref.at[pl.ds(aligned((chip * 2 + core) * rows + start, half), size)]

    def ring_copy(direction, s):
        chip = (z - s + n) % n if direction == 0 else (z + s) % n
        start, size = (0, rows) if s + 1 < steps else (direction * half, half)
        dst = block(chip, c, start, size)
        src = pooled_ref.at[pl.ds(start, size)] if s == 0 else dst
        return remote(
            src, dst, ring_send.at[direction, s], ring_recv.at[direction, s],
            right if direction == 0 else left,
        )

    def pair_copy(k, chip):
        dst = block(chip, c)
        src = pooled_ref if k == 0 else dst
        return remote(src, dst, pair_send.at[k], pair_recv.at[k], pair)

    def head(chip, core, own=False):
        span = pl.ds(aligned((chip * 2 + core) * rows, rows), rows)
        features = pooled_ref[...] if own else all_ref[span, :]
        if own:
            all_ref[span, :] = features
        preact = jnp.dot(features, first_ref[...], preferred_element_type=F32)
        preact_ref[span, :] = preact
        hidden = jax.nn.gelu(preact).astype(BF16)
        hidden_ref[span, :] = hidden
        partial_ref[span, :] = jnp.dot(hidden, second_ref[...], preferred_element_type=F32)

    started = []

    def start(copy):
        copy.start()
        started.append(copy)
        return copy

    rights = [start(ring_copy(0, 0))]
    lefts = [start(ring_copy(1, 0))]
    pairs = [(start(pair_copy(0, z)), z)]
    head(z, c, own=True)
    waited = 0
    for s in range(steps):
        rights[s].wait_recv()
        lefts[s].wait_recv()
        before = (z - 1 - s + 2 * n) % n
        after = (z + 1 + s) % n
        if s + 1 < steps:
            rights.append(start(ring_copy(0, s + 1)))
            lefts.append(start(ring_copy(1, s + 1)))
            fresh = [before, after]
        else:
            fresh = [after]
        arrived = pairs[waited:]
        waited = len(pairs)
        for chip in fresh:
            pairs.append((start(pair_copy(len(pairs), chip)), chip))
        for copy, chip in arrived:
            copy.wait_recv()
            head(chip, 1 - c)
        for chip in fresh:
            head(chip, c)
    for copy, chip in pairs[waited:]:
        copy.wait_recv()
        head(chip, 1 - c)
    for copy in started:
        copy.wait_send()


def middle_kernel(
    cycle, n, part_ref, pos_ref, grad_ref, loss_ref,
    pbuf, acc, zbuf, unit_ref, length_ref, keys, stats, escore,
    psend, precv, zsend, zrecv, ksend, krecv, ssend, srecv, gsend, grecv,
):
    group = 2 * n
    count = cycle * group
    rows, width = unit_ref.shape
    b = lax.axis_index("blk")
    g = lax.axis_index("grp")
    z, c = g // 2, g % 2
    me = b * group + g
    pair_g = z * 2 + 1 - c

    def other(k):
        device = (me + k) % count
        return {"blk": device // group, "grp": device % group}

    barrier = pltpu.get_barrier_semaphore()

    def hello(k, carry):
        pl.semaphore_signal(barrier, inc=1, device_id=other(k), device_id_type=MESH)
        return carry

    lax.fori_loop(1, count, hello, 0)
    pl.semaphore_wait(barrier, count - 1)

    started = []

    def start(copy):
        copy.start()
        started.append(copy)
        return copy

    def part(chip, core):
        return pl.ds(aligned((chip * 2 + core) * rows, rows), rows)

    order = list(range(1, n)) + [0]
    fromers = {}
    for d in order:
        fromers[d] = start(
            remote(
                part_ref.at[part((z + d) % n, 1 - c)], pbuf.at[d],
                psend.at[d], precv.at[d], {"grp": pair_g},
            )
        )
    sums = {}
    for d in order:
        fromers[d].wait_recv()
        total = part_ref[part((z + d) % n, c), :] + pbuf[d]
        acc[d] = total
        if d:
            sums[d] = start(
                remote(
                    acc.at[d], zbuf.at[d], zsend.at[d], zrecv.at[d],
                    {"grp": ((z + d) % n) * 2 + c},
                )
            )
    raw = acc[0]
    for d in range(1, n):
        sums[d].wait_recv()
        raw = raw + zbuf[d]
    length = jnp.sqrt(jnp.sum(raw * raw, axis=1, keepdims=True) + 1e-06)
    unit = raw / length
    unit_ref[...] = unit
    length_ref[...] = jnp.broadcast_to(length, length_ref.shape)
    keys[me] = unit.astype(BF16)

    def slot(e, d, core):
        return ((b - e + cycle) % cycle * n + (z - d + n) % n) * 2 + core

    sent = [0]

    def send(s, device):
        k = sent[0]
        sent[0] += 1
        return start(remote(keys.at[s], keys.at[s], ksend.at[k], krecv.at[s], device))

    def arrive(s):
        remote(keys.at[s], keys.at[s], ksend.at[0], krecv.at[s], {"grp": pair_g}).wait_recv()

    for d in range(1, n):
        send(me, {"grp": ((z + d) % n) * 2 + c})
    for e in range(1, cycle):
        send(me, {"blk": (b + e) % cycle})
    send(me, {"grp": pair_g})
    for d in range(1, n):
        s = slot(0, d, c)
        arrive(s)
        for e in range(1, cycle):
            send(s, {"blk": (b + e) % cycle})
        send(s, {"grp": pair_g})
    for d in range(n):
        for e in range(1, cycle):
            s = slot(e, d, c)
            arrive(s)
            send(s, {"grp": pair_g})
    for d in range(n):
        for e in range(cycle):
            arrive(slot(e, d, 1 - c))

    lane = 128
    per = 4
    chunk = per * rows
    row_ids = me * rows + lax.broadcasted_iota(jnp.int32, (rows, 1), 0)
    positive = pos_ref[...]
    mine = keys[me]

    def key_ids(j):
        return j * chunk + lax.broadcasted_iota(jnp.int32, (1, chunk), 1)

    def lanes(values):
        folded = values[:, :lane]
        for t in range(1, chunk // lane):
            folded = folded + values[:, t * lane : (t + 1) * lane]
        return folded

    def first_pass(j, carry):
        total, pos_score = carry
        block = keys[pl.ds(j * per, per)].reshape(chunk, width)
        scores = (
            lax.dot_general(mine, block, (((1,), (1,)), ((), ())), preferred_element_type=F32)
            * sharpness
        )
        ids = key_ids(j)
        terms = jnp.where(ids == row_ids, 0.0, jnp.exp(scores - score_top))
        escore[:, pl.ds(aligned(j * chunk, chunk), chunk)] = terms
        picked = jnp.where(ids == positive, scores, 0.0)
        return total + lanes(terms), pos_score + lanes(picked)

    zero = jnp.zeros((rows, lane), F32)
    total, pos_score = lax.fori_loop(0, count // per, first_pass, (zero, zero))
    total = jnp.sum(total, axis=1, keepdims=True)
    inverse = 1.0 / total
    term = jnp.log(total) + score_top - jnp.sum(pos_score, axis=1, keepdims=True)
    eye = lax.broadcasted_iota(jnp.int32, (rows, rows), 0) == lax.broadcasted_iota(
        jnp.int32, (rows, rows), 1
    )
    inverse_row = jnp.sum(jnp.where(eye, inverse, 0.0), axis=0, keepdims=True)
    term_row = jnp.sum(jnp.where(eye, term, 0.0), axis=0, keepdims=True)
    which = lax.broadcasted_iota(jnp.int32, (8, rows), 0)
    stats[me] = jnp.where(which == 0, inverse_row, term_row)

    def stat_copy(k, s):
        return remote(stats.at[s], stats.at[s], ssend.at[k], srecv.at[s], other(k))

    def tell(k, carry):
        stat_copy(k, me).start()
        return carry

    lax.fori_loop(1, count, tell, 0)

    def second_pass(j, gradient):
        span = pl.ds(aligned(j * chunk, chunk), chunk)
        block = keys[pl.ds(j * per, per)].reshape(chunk, width)
        paired = jnp.where(key_ids(j) == positive, 1.0, 0.0)
        weights = (escore[:, span] * inverse - paired).astype(BF16)
        return gradient + jnp.dot(weights, block, preferred_element_type=F32)

    gradient = lax.fori_loop(0, count // per, second_pass, jnp.zeros((rows, width), F32))

    def hear(k, carry):
        stat_copy(k, (me - k + count) % count).wait_recv()
        stat_copy(k, me).wait_send()
        return carry

    lax.fori_loop(1, count, hear, 0)
    loss = jnp.sum(jnp.sum(stats[:, 1, :], axis=0, keepdims=True), axis=1, keepdims=True)
    loss_ref[...] = jnp.broadcast_to(loss / (count * rows), loss_ref.shape)

    def mirror_pass(j, gradient):
        span = pl.ds(aligned(j * chunk, chunk), chunk)
        block = keys[pl.ds(j * per, per)].reshape(chunk, width)
        paired = jnp.where(key_ids(j) == positive, 1.0, 0.0)
        scale = jnp.concatenate([stats[j * per + t, 0:1, :] for t in range(per)], axis=1)
        weights = (escore[:, span] * scale - paired).astype(BF16)
        return gradient + jnp.dot(weights, block, preferred_element_type=F32)

    mirrored = lax.fori_loop(0, count // per, mirror_pass, jnp.zeros((rows, width), F32))
    sphere = (gradient + mirrored) * (sharpness / (count * rows))
    unit = unit_ref[...]
    raw_grad = (sphere - unit * jnp.sum(unit * sphere, axis=1, keepdims=True)) / length_ref[:, 0:1]
    grad_ref[part(z, c), :] = raw_grad.astype(BF16)

    def grad_copy(chip, k, q, device):
        span = part(chip, c)
        return start(remote(grad_ref.at[span], grad_ref.at[span], gsend.at[k], grecv.at[q], device))

    others = []
    for d in range(1, n):
        others.append(grad_copy(z, d, d, {"grp": ((z + d) % n) * 2 + c}))
    pairs = [grad_copy(z, n, n, {"grp": pair_g})]
    for d in range(1, n):
        others[d - 1].wait_recv()
        pairs.append(grad_copy((z - d + n) % n, n + d, n + d, {"grp": pair_g}))
    for copy in pairs:
        copy.wait_recv()
    for copy in started:
        copy.wait_send()


def reduce_kernel(
    cycle, lane_count, first_ref, second_ref, out_ref, acc, sendb, recvb,
    rs_send, rs_recv, ag_send, ag_recv,
):
    b = lax.axis_index("blk")
    stages = cycle.bit_length() - 1
    bits = [(b // (1 << t)) % 2 for t in range(stages)]
    peers = [{"blk": b + (1 - 2 * bits[t]) * (1 << t)} for t in range(stages)]
    greet(peers)
    top = first_ref.shape[0]
    total = out_ref.shape[0]
    acc[pl.ds(0, top), :] = first_ref[...]
    acc[pl.ds(top, total - top), :] = second_ref[...]
    size = total // lane_count
    orders = [
        list(range(stages)) if lane % 2 == 0 else list(range(stages))[::-1]
        for lane in range(lane_count)
    ]
    current = [lane * size for lane in range(lane_count)]
    kept = [[None] * stages for _ in range(lane_count)]
    copies = {}
    finals = {}
    started = []

    def span(start, length):
        return pl.ds(aligned(start, 16), length)

    def offset(lane, i):
        return lane * size + size - (size >> i)

    def start_reduce(lane, i):
        t = orders[lane][i]
        length = size >> (i + 1)
        away = current[lane] + (1 - bits[t]) * length
        current[lane] = current[lane] + bits[t] * length
        kept[lane][i] = current[lane]
        buffer = pl.ds(offset(lane, i), length)
        sendb[buffer, :] = acc[span(away, length), :].astype(BF16)
        copy = remote(
            sendb.at[buffer], recvb.at[buffer], rs_send.at[lane, i], rs_recv.at[lane, i], peers[t]
        )
        copy.start()
        started.append(copy)
        copies[lane, i] = copy

    def start_gather(lane, i):
        t = orders[lane][i]
        rows = out_ref.at[span(kept[lane][i], size >> (i + 1))]
        copy = remote(rows, rows, ag_send.at[lane, i], ag_recv.at[lane, i], peers[t])
        copy.start()
        started.append(copy)
        finals[lane, i] = copy

    for lane in range(lane_count):
        start_reduce(lane, 0)
    for i in range(stages):
        for lane in range(lane_count):
            copies[lane, i].wait_recv()
            length = size >> (i + 1)
            keep = span(kept[lane][i], length)
            summed = acc[keep, :] + recvb[pl.ds(offset(lane, i), length), :].astype(F32)
            if i + 1 < stages:
                acc[keep, :] = summed
                start_reduce(lane, i + 1)
            else:
                out_ref[keep, :] = summed.astype(BF16)
                start_gather(lane, i)
    for i in reversed(range(stages)):
        for lane in range(lane_count):
            finals[lane, i].wait_recv()
            if i:
                start_gather(lane, i - 1)
    for copy in started:
        copy.wait_send()


VMEM = pl.BlockSpec(memory_space=pltpu.VMEM)
DMA = pltpu.SemaphoreType.DMA


def params(number, mib=None):
    return pltpu.CompilerParams(
        collective_id=number,
        has_side_effects=True,
        vmem_limit_bytes=None if mib is None else mib << 20,
    )


def shards(frames, counts, positives, w_first, w_second):
    rows, slot_count, width = frames.shape
    cycle = lax.axis_size("blk")
    group = lax.axis_size("grp")
    n = group // 2
    count = cycle * group
    units, edge = w_second.shape
    frame_mask = (jnp.arange(slot_count, dtype=jnp.int32)[None, :] < counts[:, None]).astype(BF16)
    summed = jnp.einsum("rf,rfc->rc", frame_mask, frames, preferred_element_type=F32)
    pooled = (summed / counts[:, None].astype(F32)).astype(BF16)
    steps = n // 2
    pooled_all, preact, hidden, partial = pl.pallas_call(
        functools.partial(head_kernel, n),
        out_shape=(
            jax.ShapeDtypeStruct((group * rows, width), BF16),
            jax.ShapeDtypeStruct((group * rows, units), F32),
            jax.ShapeDtypeStruct((group * rows, units), BF16),
            jax.ShapeDtypeStruct((group * rows, edge), F32),
        ),
        in_specs=[VMEM] * 3,
        out_specs=(VMEM,) * 4,
        scratch_shapes=[DMA((2, steps)), DMA((2, steps)), DMA((n,)), DMA((n,))],
        compiler_params=params(0),
        name="head",
    )(pooled, w_first, w_second)
    group_grad, loss = pl.pallas_call(
        functools.partial(middle_kernel, cycle, n),
        out_shape=(
            jax.ShapeDtypeStruct((group * rows, edge), BF16),
            jax.ShapeDtypeStruct((8, 128), F32),
        ),
        in_specs=[VMEM] * 2,
        out_specs=(VMEM,) * 2,
        scratch_shapes=[
            pltpu.VMEM((n, rows, edge), F32),
            pltpu.VMEM((n, rows, edge), F32),
            pltpu.VMEM((n, rows, edge), F32),
            pltpu.VMEM((rows, edge), F32),
            pltpu.VMEM((rows, 128), F32),
            pltpu.VMEM((count, rows, edge), BF16),
            pltpu.VMEM((count, 8, rows), F32),
            pltpu.VMEM((rows, count * rows), F32),
            DMA((n,)), DMA((n,)), DMA((n,)), DMA((n,)),
            DMA((count,)), DMA((count,)), DMA((count,)), DMA((count,)),
            DMA((2 * n,)), DMA((2 * n,)),
        ],
        compiler_params=params(1),
        name="middle",
    )(partial, positives[:, None])
    second_grad = lax.dot_general(
        hidden, group_grad, (((0,), (0,)), ((), ())), preferred_element_type=F32
    )
    hidden_grad = lax.dot_general(
        group_grad, w_second, (((1,), (1,)), ((), ())), preferred_element_type=F32
    )
    unused, backward = jax.vjp(jax.nn.gelu, preact)
    preact_grad = backward(hidden_grad)[0].astype(BF16)
    first_grad = lax.dot_general(
        pooled_all, preact_grad, (((0,), (0,)), ((), ())), preferred_element_type=F32
    )
    fold = units // edge
    folded_rows = units // fold
    folded = jnp.concatenate(
        [second_grad[t * folded_rows : (t + 1) * folded_rows] for t in range(fold)], axis=1
    )
    total = width + folded_rows
    lane_count = 4 if total % (4 * cycle * 16) == 0 else 2
    stages = cycle.bit_length() - 1
    summed = pl.pallas_call(
        functools.partial(reduce_kernel, cycle, lane_count),
        out_shape=jax.ShapeDtypeStruct((total, units), BF16),
        in_specs=[VMEM] * 2,
        out_specs=VMEM,
        scratch_shapes=[
            pltpu.VMEM((total, units), F32),
            pltpu.VMEM((total, units), BF16),
            pltpu.VMEM((total, units), BF16),
            DMA((lane_count, stages)), DMA((lane_count, stages)),
            DMA((lane_count, stages)), DMA((lane_count, stages)),
        ],
        compiler_params=params(2),
        name="reduce",
    )(first_grad, folded)
    first_out = summed[:width].astype(F32)
    second_out = jnp.concatenate(
        [summed[width:, t * edge : (t + 1) * edge] for t in range(fold)], axis=0
    ).astype(F32)
    return (loss[0, 0], first_out, second_out)


def solution(mesh):
    return jax.shard_map(
        shards,
        mesh=mesh,
        in_specs=(
            P(("blk", "grp"), None, None),
            P(("blk", "grp")),
            P(("blk", "grp")),
            P(None, "grp"),
            P("grp", None),
        ),
        out_specs=(P(), P(None, "grp"), P("grp", None)),
        check_vma=False,
    )
```

```python
import functools

import jax
import jax.numpy as jnp
from jax import lax
from jax.experimental import pallas as pl
from jax.experimental.pallas import tpu as pltpu
from jax.sharding import PartitionSpec as P

sharpness = 20.0
score_top = 20.0
MESH = pl.DeviceIdType.MESH
F32 = jnp.float32
BF16 = jnp.bfloat16


def aligned(start, step):
    return pl.multiple_of(start, step)


def greet(partners):
    barrier = pltpu.get_barrier_semaphore()
    for device in partners:
        pl.semaphore_signal(barrier, inc=1, device_id=device, device_id_type=MESH)
    pl.semaphore_wait(barrier, len(partners))


def remote(src, dst, send_sem, recv_sem, device):
    return pltpu.make_async_remote_copy(
        src_ref=src,
        dst_ref=dst,
        send_sem=send_sem,
        recv_sem=recv_sem,
        device_id=device,
        device_id_type=MESH,
    )


def head_kernel(
    n, pooled_ref, first_hbm, second_ref, all_out, preact_out, hidden_out, partial_ref,
    first_ref, all_ref, preact_ref, hidden_ref,
    line_send, line_recv, pair_send, pair_recv, load_sem, store_sem,
):
    rows = pooled_ref.shape[0]
    parts = line_send.shape[2]
    piece = rows // parts
    g = lax.axis_index("grp")
    z, c = g // 2, g % 2
    pair = {"grp": z * 2 + 1 - c}
    has_right, has_left = z < n - 1, z > 0
    ways = (
        ({"grp": g + 2}, has_right, lambda s: z - s, lambda s: z - 1 - s >= 0),
        ({"grp": g - 2}, has_left, lambda s: z + s, lambda s: z + 1 + s < n),
    )
    load = pltpu.make_async_copy(first_hbm, first_ref, load_sem)
    load.start()

    barrier = pltpu.get_barrier_semaphore()
    pl.semaphore_signal(barrier, inc=1, device_id=pair, device_id_type=MESH)
    for device, exists, _, _ in ways:

        @pl.when(exists)
        def _():
            pl.semaphore_signal(barrier, inc=1, device_id=device, device_id_type=MESH)

    pl.semaphore_wait(barrier, 1 + has_right.astype(jnp.int32) + has_left.astype(jnp.int32))

    def rows_of(chip, core):
        return pl.ds(aligned((chip * 2 + core) * rows, rows), rows)

    def spot(chip, q):
        return all_ref.at[pl.ds(aligned((chip * 2 + c) * rows + q * piece, piece), piece)]

    def line_copy(way, s, q, incoming=False):
        device, _, chip, _ = ways[way]
        dst = spot(chip(s + 1) if incoming else chip(s), q)
        src = pooled_ref.at[pl.ds(q * piece, piece)] if s == 0 and not incoming else dst
        return remote(src, dst, line_send.at[way, s, q], line_recv.at[way, s, q], device)

    def pair_copy(k, chip, q):
        dst = spot(chip, q)
        src = pooled_ref.at[pl.ds(q * piece, piece)] if k == 0 else dst
        return remote(src, dst, pair_send.at[k, q], pair_recv.at[k, q], pair)

    def stores(chip, core):
        span = rows_of(chip, core)
        which = chip * 2 + core
        return [
            pltpu.make_async_copy(source.at[span], target.at[span], store_sem.at[i, which])
            for i, (source, target) in enumerate(
                ((all_ref, all_out), (preact_ref, preact_out), (hidden_ref, hidden_out))
            )
        ]

    def head(chip, core, own=False):
        span = rows_of(chip, core)
        features = pooled_ref[...] if own else all_ref[span, :]
        if own:
            all_ref[span, :] = features
        preact = jnp.dot(features, first_ref[...], preferred_element_type=F32)
        preact_ref[span, :] = preact
        hidden = jax.nn.gelu(preact).astype(BF16)
        hidden_ref[span, :] = hidden
        partial_ref[span, :] = jnp.dot(hidden, second_ref[...], preferred_element_type=F32)
        for copy in stores(chip, core):
            copy.start()

    def pair_head(k, chip):
        for q in range(parts):
            pair_copy(k, chip, q).wait_recv()
        head(chip, 1 - c)

    for q in range(parts):
        for way in range(2):

            @pl.when(ways[way][1])
            def _():
                line_copy(way, 0, q).start()

        pair_copy(0, z, q).start()
    load.wait()
    head(z, c, own=True)

    def key_of(way, s):
        return 1 + s if way == 0 else n + s

    for s in range(n - 1):
        for q in range(parts):
            for way in range(2):
                _, exists, chip, arrives = ways[way]

                @pl.when(arrives(s))
                def _():
                    line_copy(way, s, q, incoming=True).wait_recv()
                    if s + 1 < n - 1:

                        @pl.when(exists)
                        def _():
                            line_copy(way, s + 1, q).start()

                    pair_copy(key_of(way, s), chip(s + 1), q).start()

        if s == 0:
            pair_head(0, z)
        for way in range(2):
            _, _, chip, arrives = ways[way]
            if s:

                @pl.when(arrives(s - 1))
                def _():
                    pair_head(key_of(way, s - 1), chip(s))

            @pl.when(arrives(s))
            def _():
                head(chip(s + 1), c)

    for way in range(2):
        _, exists, chip, arrives = ways[way]

        @pl.when(arrives(n - 2))
        def _():
            pair_head(key_of(way, n - 2), chip(n - 1))

    for q in range(parts):
        pair_copy(0, z, q).wait_send()
        for way in range(2):
            _, exists, chip, arrives = ways[way]

            @pl.when(exists)
            def _():
                line_copy(way, 0, q).wait_send()

            for s in range(n - 1):

                @pl.when(arrives(s))
                def _():
                    pair_copy(key_of(way, s), chip(s + 1), q).wait_send()
                    if s + 1 < n - 1:

                        @pl.when(exists)
                        def _():
                            line_copy(way, s + 1, q).wait_send()

    for chip in range(n):
        for core in range(2):
            for copy in stores(chip, core):
                copy.wait()


def middle_kernel(
    cycle, n, part_ref, pos_ref, grad_ref, loss_ref,
    pbuf, acc, zbuf, unit_ref, length_ref, keys, stats, escore,
    psend, precv, zsend, zrecv, ksend, krecv, ssend, srecv, gsend, grecv,
):
    group = 2 * n
    count = cycle * group
    rows, width = unit_ref.shape
    b = lax.axis_index("blk")
    g = lax.axis_index("grp")
    z, c = g // 2, g % 2
    me = b * group + g
    pair_g = z * 2 + 1 - c

    def other(k):
        device = (me + k) % count
        return {"blk": device // group, "grp": device % group}

    barrier = pltpu.get_barrier_semaphore()

    def hello(k, carry):
        pl.semaphore_signal(barrier, inc=1, device_id=other(k), device_id_type=MESH)
        return carry

    lax.fori_loop(1, count, hello, 0)
    pl.semaphore_wait(barrier, count - 1)

    started = []

    def start(copy):
        copy.start()
        started.append(copy)
        return copy

    def part(chip, core):
        return pl.ds(aligned((chip * 2 + core) * rows, rows), rows)

    order = list(range(1, n)) + [0]
    fromers = {}
    for d in order:
        fromers[d] = start(
            remote(
                part_ref.at[part((z + d) % n, 1 - c)], pbuf.at[d],
                psend.at[d], precv.at[d], {"grp": pair_g},
            )
        )
    sums = {}
    for d in order:
        fromers[d].wait_recv()
        total = part_ref[part((z + d) % n, c), :] + pbuf[d]
        acc[d] = total
        if d:
            sums[d] = start(
                remote(
                    acc.at[d], zbuf.at[d], zsend.at[d], zrecv.at[d],
                    {"grp": ((z + d) % n) * 2 + c},
                )
            )
    raw = acc[0]
    for d in range(1, n):
        sums[d].wait_recv()
        raw = raw + zbuf[d]
    length = jnp.sqrt(jnp.sum(raw * raw, axis=1, keepdims=True) + 1e-06)
    unit = raw / length
    unit_ref[...] = unit
    length_ref[...] = jnp.broadcast_to(length, length_ref.shape)
    keys[me] = unit.astype(BF16)

    def slot(e, d, core):
        return ((b - e + cycle) % cycle * n + (z - d + n) % n) * 2 + core

    sent = [0]

    def send(s, device):
        k = sent[0]
        sent[0] += 1
        return start(remote(keys.at[s], keys.at[s], ksend.at[k], krecv.at[s], device))

    def arrive(s):
        remote(keys.at[s], keys.at[s], ksend.at[0], krecv.at[s], {"grp": pair_g}).wait_recv()

    for d in range(1, n):
        send(me, {"grp": ((z + d) % n) * 2 + c})
    for e in range(1, cycle):
        send(me, {"blk": (b + e) % cycle})
    send(me, {"grp": pair_g})
    for d in range(1, n):
        s = slot(0, d, c)
        arrive(s)
        for e in range(1, cycle):
            send(s, {"blk": (b + e) % cycle})
        send(s, {"grp": pair_g})
    lane = 128
    per = 4
    chunk = per * rows
    row_ids = me * rows + lax.broadcasted_iota(jnp.int32, (rows, 1), 0)
    eye = lax.broadcasted_iota(jnp.int32, (rows, rows), 0) == lax.broadcasted_iota(
        jnp.int32, (rows, rows), 1
    )
    positive = jnp.sum(jnp.where(eye, pos_ref[...].astype(F32), 0.0), axis=1, keepdims=True)
    positive = positive.astype(jnp.int32)
    mine = keys[me]

    def key_ids(j):
        return j * chunk + lax.broadcasted_iota(jnp.int32, (1, chunk), 1)

    def lanes(values):
        folded = values[:, :lane]
        for t in range(1, chunk // lane):
            folded = folded + values[:, t * lane : (t + 1) * lane]
        return folded

    def first_pass(j, carry):
        total, pos_score = carry
        block = keys[pl.ds(j * per, per)].reshape(chunk, width)
        scores = (
            lax.dot_general(mine, block, (((1,), (1,)), ((), ())), preferred_element_type=F32)
            * sharpness
        )
        ids = key_ids(j)
        terms = jnp.where(ids == row_ids, 0.0, jnp.exp(scores - score_top))
        escore[:, pl.ds(aligned(j * chunk, chunk), chunk)] = terms
        picked = jnp.where(ids == positive, scores, 0.0)
        return total + lanes(terms), pos_score + lanes(picked)

    zero = jnp.zeros((rows, lane), F32)
    carry = (zero, zero)
    chunks = group // per
    for e in range(cycle):
        if e == 1:
            for other_e in range(1, cycle):
                for d in range(n):
                    s = slot(other_e, d, c)
                    arrive(s)
                    send(s, {"grp": pair_g})
        for d in range(n):
            arrive(slot(e, d, 1 - c))
        base = (b - e + cycle) % cycle * chunks
        carry = lax.fori_loop(base, base + chunks, first_pass, carry)
    total, pos_score = carry
    total = jnp.sum(total, axis=1, keepdims=True)
    inverse = 1.0 / total
    term = jnp.log(total) + score_top - jnp.sum(pos_score, axis=1, keepdims=True)
    inverse_row = jnp.sum(jnp.where(eye, inverse, 0.0), axis=0, keepdims=True)
    term_row = jnp.sum(jnp.where(eye, term, 0.0), axis=0, keepdims=True)
    which = lax.broadcasted_iota(jnp.int32, (8, rows), 0)
    stats[me] = jnp.where(which == 0, inverse_row, term_row)

    def stat_copy(k, s):
        return remote(stats.at[s], stats.at[s], ssend.at[k], srecv.at[s], other(k))

    def tell(k, carry):
        stat_copy(k, me).start()
        return carry

    lax.fori_loop(1, count, tell, 0)

    def second_pass(j, gradient):
        span = pl.ds(aligned(j * chunk, chunk), chunk)
        block = keys[pl.ds(j * per, per)].reshape(chunk, width)
        paired = jnp.where(key_ids(j) == positive, 1.0, 0.0)
        weights = (escore[:, span] * inverse - paired).astype(BF16)
        return gradient + jnp.dot(weights, block, preferred_element_type=F32)

    gradient = lax.fori_loop(0, count // per, second_pass, jnp.zeros((rows, width), F32))

    def hear(k, carry):
        stat_copy(k, (me - k + count) % count).wait_recv()
        stat_copy(k, me).wait_send()
        return carry

    lax.fori_loop(1, count, hear, 0)
    loss_ref[0, 0] = jnp.sum(stats[:, 1, :]) / (count * rows)

    def mirror_pass(j, gradient):
        span = pl.ds(aligned(j * chunk, chunk), chunk)
        block = keys[pl.ds(j * per, per)].reshape(chunk, width)
        paired = jnp.where(key_ids(j) == positive, 1.0, 0.0)
        scale = jnp.concatenate([stats[j * per + t, 0:1, :] for t in range(per)], axis=1)
        weights = (escore[:, span] * scale - paired).astype(BF16)
        return gradient + jnp.dot(weights, block, preferred_element_type=F32)

    mirrored = lax.fori_loop(0, count // per, mirror_pass, jnp.zeros((rows, width), F32))
    sphere = (gradient + mirrored) * (sharpness / (count * rows))
    unit = unit_ref[...]
    raw_grad = (sphere - unit * jnp.sum(unit * sphere, axis=1, keepdims=True)) / length_ref[:, 0:1]
    grad_ref[part(z, c), :] = raw_grad.astype(BF16)

    def grad_copy(chip, k, q, device):
        span = part(chip, c)
        return start(remote(grad_ref.at[span], grad_ref.at[span], gsend.at[k], grecv.at[q], device))

    others = []
    for d in range(1, n):
        others.append(grad_copy(z, d, d, {"grp": ((z + d) % n) * 2 + c}))
    pairs = [grad_copy(z, n, n, {"grp": pair_g})]
    for d in range(1, n):
        others[d - 1].wait_recv()
        pairs.append(grad_copy((z - d + n) % n, n + d, n + d, {"grp": pair_g}))
    for copy in pairs:
        copy.wait_recv()
    for copy in started:
        copy.wait_send()


def reduce_kernel(
    cycle, lane_count, grad_ref, second_ref, pooled_hbm, preact_hbm, hidden_hbm, out_ref,
    pooled_ref, preact_ref, hidden_ref, back_ref, second_grad, acc, sendb, recvb,
    load_sem, rs_send, rs_recv, ag_send, ag_recv,
):
    loads = [
        pltpu.make_async_copy(source, target, load_sem.at[i])
        for i, (source, target) in enumerate(
            ((preact_hbm, preact_ref), (hidden_hbm, hidden_ref), (pooled_hbm, pooled_ref))
        )
    ]
    for load in loads:
        load.start()
    b = lax.axis_index("blk")
    stages = cycle.bit_length() - 1
    bits = [(b // (1 << t)) % 2 for t in range(stages)]
    peers = [{"blk": b + (1 - 2 * bits[t]) * (1 << t)} for t in range(stages)]
    greet(peers)
    clips = preact_ref.shape[0]
    edge = second_ref.shape[1]
    fold = second_ref.shape[0] // edge
    total = out_ref.shape[0]
    size = total // lane_count
    unit = size // cycle
    top = pooled_ref.shape[1] // (lane_count * cycle)
    low = unit - top
    loads[0].wait()
    step = 128

    def back(i, carry):
        span = pl.ds(aligned(i * step, step), step)
        hidden_grad = lax.dot_general(
            grad_ref[span, :], second_ref[...], (((1,), (1,)), ((), ())),
            preferred_element_type=F32,
        )
        unused, backward = jax.vjp(jax.nn.gelu, preact_ref[span, :])
        back_ref[span, :] = backward(hidden_grad)[0].astype(BF16)
        return carry

    lax.fori_loop(0, clips // step, back, 0)
    loads[1].wait()
    across = (((0,), (0,)), ((), ()))
    second_grad[...] = lax.dot_general(
        hidden_ref[...], grad_ref[...], across, preferred_element_type=F32
    )
    loads[2].wait()

    def produce(lane):
        wide = top * cycle
        first = lax.dot_general(
            pooled_ref[:, lane * wide : (lane + 1) * wide], back_ref[...], across,
            preferred_element_type=F32,
        )
        for j in range(cycle):
            at = lane * size + j * unit
            acc[pl.ds(at, top), :] = first[j * top : (j + 1) * top]
            for t in range(fold):
                row = t * edge + (lane * cycle + j) * low
                acc[pl.ds(at + top, low), t * edge : (t + 1) * edge] = second_grad[
                    pl.ds(row, low), :
                ]

    orders = [
        list(range(stages)) if lane % 2 == 0 else list(range(stages))[::-1]
        for lane in range(lane_count)
    ]
    current = [lane * size for lane in range(lane_count)]
    kept = [[None] * stages for _ in range(lane_count)]
    copies = {}
    finals = {}
    started = []

    def span(start, length):
        return pl.ds(aligned(start, 16), length)

    def offset(lane, i):
        return lane * size + size - (size >> i)

    def start_reduce(lane, i):
        t = orders[lane][i]
        length = size >> (i + 1)
        away = current[lane] + (1 - bits[t]) * length
        current[lane] = current[lane] + bits[t] * length
        kept[lane][i] = current[lane]
        buffer = pl.ds(offset(lane, i), length)
        sendb[buffer, :] = acc[span(away, length), :].astype(BF16)
        copy = remote(
            sendb.at[buffer], recvb.at[buffer], rs_send.at[lane, i], rs_recv.at[lane, i], peers[t]
        )
        copy.start()
        started.append(copy)
        copies[lane, i] = copy

    def start_gather(lane, i):
        t = orders[lane][i]
        rows = out_ref.at[span(kept[lane][i], size >> (i + 1))]
        copy = remote(rows, rows, ag_send.at[lane, i], ag_recv.at[lane, i], peers[t])
        copy.start()
        started.append(copy)
        finals[lane, i] = copy

    for lane in range(lane_count):
        produce(lane)
        start_reduce(lane, 0)
    for i in range(stages):
        for lane in range(lane_count):
            copies[lane, i].wait_recv()
            length = size >> (i + 1)
            keep = span(kept[lane][i], length)
            summed = acc[keep, :] + recvb[pl.ds(offset(lane, i), length), :].astype(F32)
            if i + 1 < stages:
                acc[keep, :] = summed
                start_reduce(lane, i + 1)
            else:
                out_ref[keep, :] = summed.astype(BF16)
                start_gather(lane, i)
    for i in reversed(range(stages)):
        for lane in range(lane_count):
            finals[lane, i].wait_recv()
            if i:
                start_gather(lane, i - 1)
    for copy in started:
        copy.wait_send()


def tail_kernel(unit, fold, sum_ref, loss_ref, first_ref, second_ref, out_ref):
    block = sum_ref[...].astype(F32)
    low = second_ref.shape[1] // (block.shape[0] // unit)
    edge = second_ref.shape[2]
    top = unit - low
    for j in range(block.shape[0] // unit):
        first_ref[j * top : (j + 1) * top, :] = block[j * unit : j * unit + top]
        for t in range(fold):
            second_ref[t, j * low : (j + 1) * low, :] = block[
                j * unit + top : (j + 1) * unit, t * edge : (t + 1) * edge
            ]
    out_ref[0, 0] = loss_ref[0, 0]


VMEM = pl.BlockSpec(memory_space=pltpu.VMEM)
SMEM = pl.BlockSpec(memory_space=pltpu.SMEM)
ANY = pl.BlockSpec(memory_space=pl.ANY)
DMA = pltpu.SemaphoreType.DMA


def params(number, mib=None):
    return pltpu.CompilerParams(
        collective_id=number,
        has_side_effects=True,
        vmem_limit_bytes=None if mib is None else mib << 20,
    )


def shards(frames, counts, positives, w_first, w_second):
    rows, slot_count, width = frames.shape
    cycle = lax.axis_size("blk")
    group = lax.axis_size("grp")
    n = group // 2
    count = cycle * group
    units, edge = w_second.shape
    frame_mask = (jnp.arange(slot_count, dtype=jnp.int32)[None, :] < counts[:, None]).astype(BF16)
    summed = jnp.einsum("rf,rfc->rc", frame_mask, frames, preferred_element_type=F32)
    pooled = (summed / counts[:, None].astype(F32)).astype(BF16)
    pooled_all, preact, hidden, partial = pl.pallas_call(
        functools.partial(head_kernel, n),
        out_shape=(
            jax.ShapeDtypeStruct((group * rows, width), BF16),
            jax.ShapeDtypeStruct((group * rows, units), F32),
            jax.ShapeDtypeStruct((group * rows, units), BF16),
            jax.ShapeDtypeStruct((group * rows, edge), F32),
        ),
        in_specs=[VMEM, ANY, VMEM],
        out_specs=(ANY, ANY, ANY, VMEM),
        scratch_shapes=[
            pltpu.VMEM((width, units), BF16),
            pltpu.VMEM((group * rows, width), BF16),
            pltpu.VMEM((group * rows, units), F32),
            pltpu.VMEM((group * rows, units), BF16),
            DMA((2, n, 2)), DMA((2, n, 2)), DMA((2 * n, 2)), DMA((2 * n, 2)),
            DMA, DMA((3, group)),
        ],
        compiler_params=params(0),
        name="head",
    )(pooled, w_first, w_second)
    group_grad, loss = pl.pallas_call(
        functools.partial(middle_kernel, cycle, n),
        out_shape=(
            jax.ShapeDtypeStruct((group * rows, edge), BF16),
            jax.ShapeDtypeStruct((1, 1), F32),
        ),
        in_specs=[VMEM] * 2,
        out_specs=(VMEM, SMEM),
        scratch_shapes=[
            pltpu.VMEM((n, rows, edge), F32),
            pltpu.VMEM((n, rows, edge), F32),
            pltpu.VMEM((n, rows, edge), F32),
            pltpu.VMEM((rows, edge), F32),
            pltpu.VMEM((rows, 128), F32),
            pltpu.VMEM((count, rows, edge), BF16),
            pltpu.VMEM((count, 8, rows), F32),
            pltpu.VMEM((rows, count * rows), F32),
            DMA((n,)), DMA((n,)), DMA((n,)), DMA((n,)),
            DMA((count,)), DMA((count,)), DMA((count,)), DMA((count,)),
            DMA((2 * n,)), DMA((2 * n,)),
        ],
        compiler_params=params(1),
        name="middle",
    )(partial, positives[None, :])
    fold = units // edge
    total = width + units // fold
    lane_count = 4 if units // fold % (4 * cycle * 16) == 0 else 2
    stages = cycle.bit_length() - 1
    links = (lane_count, stages)
    summed = pl.pallas_call(
        functools.partial(reduce_kernel, cycle, lane_count),
        out_shape=jax.ShapeDtypeStruct((total, units), BF16),
        in_specs=[VMEM, VMEM, ANY, ANY, ANY],
        out_specs=VMEM,
        scratch_shapes=[
            pltpu.VMEM((group * rows, width), BF16),
            pltpu.VMEM((group * rows, units), F32),
            pltpu.VMEM((group * rows, units), BF16),
            pltpu.VMEM((group * rows, units), BF16),
            pltpu.VMEM((units, edge), F32),
            pltpu.VMEM((total, units), F32),
            pltpu.VMEM((total, units), BF16),
            pltpu.VMEM((total, units), BF16),
            DMA((3,)), DMA(links), DMA(links), DMA(links), DMA(links),
        ],
        compiler_params=params(2),
        name="reduce",
    )(group_grad, w_second, pooled_all, preact, hidden)
    unit = total // (lane_count * cycle)
    tiles = lane_count * cycle // 2
    first_out, second_out, loss = pl.pallas_call(
        functools.partial(tail_kernel, unit, fold),
        grid=(tiles,),
        out_shape=(
            jax.ShapeDtypeStruct((width, units), F32),
            jax.ShapeDtypeStruct((fold, units // fold, edge), F32),
            jax.ShapeDtypeStruct((1, 1), F32),
        ),
        in_specs=[pl.BlockSpec((2 * unit, units), lambda i: (i, 0)), SMEM],
        out_specs=(
            pl.BlockSpec((width // tiles, units), lambda i: (i, 0)),
            pl.BlockSpec((fold, units // fold // tiles, edge), lambda i: (0, i, 0)),
            SMEM,
        ),
        name="tail",
    )(summed, loss)
    return (loss.reshape(()), first_out, second_out.reshape(units, edge))


def solution(mesh):
    return jax.shard_map(
        shards,
        mesh=mesh,
        in_specs=(
            P(("blk", "grp"), None, None),
            P(("blk", "grp")),
            P(("blk", "grp")),
            P(None, "grp"),
            P("grp", None),
        ),
        out_specs=(P(), P(None, "grp"), P("grp", None)),
        check_vma=False,
    )
```

```python
import functools

import jax
import jax.numpy as jnp
from jax import lax
from jax.experimental import pallas as pl
from jax.experimental.pallas import tpu as pltpu
from jax.sharding import PartitionSpec as P

sharpness = 20.0
score_top = 20.0
MESH = pl.DeviceIdType.MESH
F32 = jnp.float32
BF16 = jnp.bfloat16


def aligned(start, step):
    return pl.multiple_of(start, step)


def greet(partners):
    barrier = pltpu.get_barrier_semaphore()
    for device in partners:
        pl.semaphore_signal(barrier, inc=1, device_id=device, device_id_type=MESH)
    pl.semaphore_wait(barrier, len(partners))


def remote(src, dst, send_sem, recv_sem, device):
    return pltpu.make_async_remote_copy(
        src_ref=src,
        dst_ref=dst,
        send_sem=send_sem,
        recv_sem=recv_sem,
        device_id=device,
        device_id_type=MESH,
    )


def head_kernel(
    n, pooled_ref, first_hbm, second_ref, all_out, preact_out, hidden_out, partial_ref,
    first_ref, all_ref, preact_ref, hidden_ref,
    line_send, line_recv, pair_send, pair_recv, load_sem, store_sem,
):
    rows = pooled_ref.shape[0]
    parts = line_send.shape[2]
    piece = rows // parts
    g = lax.axis_index("grp")
    z, c = g // 2, g % 2
    pair = {"grp": z * 2 + 1 - c}
    has_right, has_left = z < n - 1, z > 0
    ways = (
        ({"grp": g + 2}, has_right, lambda s: z - s, lambda s: z - 1 - s >= 0),
        ({"grp": g - 2}, has_left, lambda s: z + s, lambda s: z + 1 + s < n),
    )
    load = pltpu.make_async_copy(first_hbm, first_ref, load_sem)
    load.start()

    barrier = pltpu.get_barrier_semaphore()
    pl.semaphore_signal(barrier, inc=1, device_id=pair, device_id_type=MESH)
    for device, exists, _, _ in ways:

        @pl.when(exists)
        def _():
            pl.semaphore_signal(barrier, inc=1, device_id=device, device_id_type=MESH)

    pl.semaphore_wait(barrier, 1 + has_right.astype(jnp.int32) + has_left.astype(jnp.int32))

    def rows_of(chip):
        return pl.ds(aligned(chip * 2 * rows, 2 * rows), 2 * rows)

    def spot(chip, q):
        return all_ref.at[pl.ds(aligned((chip * 2 + c) * rows + q * piece, piece), piece)]

    def line_copy(way, s, q, incoming=False):
        device, _, chip, _ = ways[way]
        dst = spot(chip(s + 1) if incoming else chip(s), q)
        src = pooled_ref.at[pl.ds(q * piece, piece)] if s == 0 and not incoming else dst
        return remote(src, dst, line_send.at[way, s, q], line_recv.at[way, s, q], device)

    def pair_copy(k, chip, q):
        dst = spot(chip, q)
        src = pooled_ref.at[pl.ds(q * piece, piece)] if k == 0 else dst
        return remote(src, dst, pair_send.at[k, q], pair_recv.at[k, q], pair)

    def stores(chip):
        span = rows_of(chip)
        return [
            pltpu.make_async_copy(source.at[span], target.at[span], store_sem.at[i, chip])
            for i, (source, target) in enumerate(
                ((all_ref, all_out), (preact_ref, preact_out), (hidden_ref, hidden_out))
            )
        ]

    def head(k, chip):
        for q in range(parts):
            pair_copy(k, chip, q).wait_recv()
        span = rows_of(chip)
        preact = jnp.dot(all_ref[span, :], first_ref[...], preferred_element_type=F32)
        preact_ref[span, :] = preact
        hidden = jax.nn.gelu(preact).astype(BF16)
        hidden_ref[span, :] = hidden
        partial_ref[span, :] = jnp.dot(hidden, second_ref[...], preferred_element_type=F32)
        for copy in stores(chip):
            copy.start()

    for q in range(parts):
        for way in range(2):

            @pl.when(ways[way][1])
            def _():
                line_copy(way, 0, q).start()

        pair_copy(0, z, q).start()
    all_ref[pl.ds(aligned(g * rows, rows), rows), :] = pooled_ref[...]
    load.wait()

    def key_of(way, s):
        return 1 + s if way == 0 else n + s

    for s in range(n - 1):
        for q in range(parts):
            for way in range(2):
                _, exists, chip, arrives = ways[way]

                @pl.when(arrives(s))
                def _():
                    line_copy(way, s, q, incoming=True).wait_recv()
                    if s + 1 < n - 1:

                        @pl.when(exists)
                        def _():
                            line_copy(way, s + 1, q).start()

                    pair_copy(key_of(way, s), chip(s + 1), q).start()

        if s == 0:
            head(0, z)
        else:
            for way in range(2):

                @pl.when(ways[way][3](s - 1))
                def _():
                    head(key_of(way, s - 1), ways[way][2](s))

    for way in range(2):

        @pl.when(ways[way][3](n - 2))
        def _():
            head(key_of(way, n - 2), ways[way][2](n - 1))

    for q in range(parts):
        pair_copy(0, z, q).wait_send()
        for way in range(2):
            _, exists, chip, arrives = ways[way]

            @pl.when(exists)
            def _():
                line_copy(way, 0, q).wait_send()

            for s in range(n - 1):

                @pl.when(arrives(s))
                def _():
                    pair_copy(key_of(way, s), chip(s + 1), q).wait_send()
                    if s + 1 < n - 1:

                        @pl.when(exists)
                        def _():
                            line_copy(way, s + 1, q).wait_send()

    for chip in range(n):
        for copy in stores(chip):
            copy.wait()


def middle_kernel(
    cycle, n, part_ref, pos_ref, preact_hbm, grad_ref, loss_ref, slope_out,
    preact_ref, move_sem,
    pbuf, acc, zbuf, unit_ref, length_ref, keys, stats, escore,
    psend, precv, zsend, zrecv, ksend, krecv, ssend, srecv, gsend, grecv,
):
    group = 2 * n
    count = cycle * group
    rows, width = unit_ref.shape
    load = pltpu.make_async_copy(preact_hbm, preact_ref, move_sem.at[0])
    load.start()
    b = lax.axis_index("blk")
    g = lax.axis_index("grp")
    z, c = g // 2, g % 2
    me = b * group + g
    pair_g = z * 2 + 1 - c

    def other(k):
        device = (me + k) % count
        return {"blk": device // group, "grp": device % group}

    barrier = pltpu.get_barrier_semaphore()

    def hello(k, carry):
        pl.semaphore_signal(barrier, inc=1, device_id=other(k), device_id_type=MESH)
        return carry

    lax.fori_loop(1, count, hello, 0)
    pl.semaphore_wait(barrier, count - 1)

    started = []

    def start(copy):
        copy.start()
        started.append(copy)
        return copy

    def part(chip, core):
        return pl.ds(aligned((chip * 2 + core) * rows, rows), rows)

    order = list(range(1, n)) + [0]
    fromers = {}
    for d in order:
        fromers[d] = start(
            remote(
                part_ref.at[part((z + d) % n, 1 - c)], pbuf.at[d],
                psend.at[d], precv.at[d], {"grp": pair_g},
            )
        )
    sums = {}
    for d in order:
        fromers[d].wait_recv()
        total = part_ref[part((z + d) % n, c), :] + pbuf[d]
        acc[d] = total
        if d:
            sums[d] = start(
                remote(
                    acc.at[d], zbuf.at[d], zsend.at[d], zrecv.at[d],
                    {"grp": ((z + d) % n) * 2 + c},
                )
            )
    load.wait()

    def slope(i, carry):
        span = pl.ds(aligned(i * rows, rows), rows)
        values = preact_ref[span, :]
        unused, backward = jax.vjp(jax.nn.gelu, values)
        preact_ref[span, :] = backward(jnp.ones_like(values))[0]
        return carry

    lax.fori_loop(0, group, slope, 0)
    store = pltpu.make_async_copy(preact_ref, slope_out, move_sem.at[1])
    store.start()
    raw = acc[0]
    for d in range(1, n):
        sums[d].wait_recv()
        raw = raw + zbuf[d]
    length = jnp.sqrt(jnp.sum(raw * raw, axis=1, keepdims=True) + 1e-06)
    unit = raw / length
    unit_ref[...] = unit
    length_ref[...] = jnp.broadcast_to(length, length_ref.shape)
    keys[me] = unit.astype(BF16)

    def slot(e, d, core):
        return ((b - e + cycle) % cycle * n + (z - d + n) % n) * 2 + core

    sent = [0]

    def send(s, device):
        k = sent[0]
        sent[0] += 1
        return start(remote(keys.at[s], keys.at[s], ksend.at[k], krecv.at[s], device))

    def arrive(s):
        remote(keys.at[s], keys.at[s], ksend.at[0], krecv.at[s], {"grp": pair_g}).wait_recv()

    for d in range(1, n):
        send(me, {"grp": ((z + d) % n) * 2 + c})
    for e in range(1, cycle):
        send(me, {"blk": (b + e) % cycle})
    send(me, {"grp": pair_g})
    for d in range(1, n):
        s = slot(0, d, c)
        arrive(s)
        for e in range(1, cycle):
            send(s, {"blk": (b + e) % cycle})
        send(s, {"grp": pair_g})
    lane = 128
    per = 4
    chunk = per * rows
    row_ids = me * rows + lax.broadcasted_iota(jnp.int32, (rows, 1), 0)
    eye = lax.broadcasted_iota(jnp.int32, (rows, rows), 0) == lax.broadcasted_iota(
        jnp.int32, (rows, rows), 1
    )
    positive = jnp.sum(jnp.where(eye, pos_ref[...].astype(F32), 0.0), axis=1, keepdims=True)
    positive = positive.astype(jnp.int32)
    mine = keys[me]

    def key_ids(j):
        return j * chunk + lax.broadcasted_iota(jnp.int32, (1, chunk), 1)

    def lanes(values):
        folded = values[:, :lane]
        for t in range(1, chunk // lane):
            folded = folded + values[:, t * lane : (t + 1) * lane]
        return folded

    def first_pass(j, carry):
        total, pos_score = carry
        block = keys[pl.ds(j * per, per)].reshape(chunk, width)
        scores = (
            lax.dot_general(mine, block, (((1,), (1,)), ((), ())), preferred_element_type=F32)
            * sharpness
        )
        ids = key_ids(j)
        terms = jnp.where(ids == row_ids, 0.0, jnp.exp(scores - score_top))
        escore[:, pl.ds(aligned(j * chunk, chunk), chunk)] = terms
        picked = jnp.where(ids == positive, scores, 0.0)
        return total + lanes(terms), pos_score + lanes(picked)

    zero = jnp.zeros((rows, lane), F32)
    carry = (zero, zero)
    chunks = group // per
    for e in range(cycle):
        if e == 1:
            for other_e in range(1, cycle):
                for d in range(n):
                    s = slot(other_e, d, c)
                    arrive(s)
                    send(s, {"grp": pair_g})
        for d in range(n):
            arrive(slot(e, d, 1 - c))
        base = (b - e + cycle) % cycle * chunks
        carry = lax.fori_loop(base, base + chunks, first_pass, carry)
    total, pos_score = carry
    total = jnp.sum(total, axis=1, keepdims=True)
    inverse = 1.0 / total
    term = jnp.log(total) + score_top - jnp.sum(pos_score, axis=1, keepdims=True)
    inverse_row = jnp.sum(jnp.where(eye, inverse, 0.0), axis=0, keepdims=True)
    term_row = jnp.sum(jnp.where(eye, term, 0.0), axis=0, keepdims=True)
    which = lax.broadcasted_iota(jnp.int32, (8, rows), 0)
    stats[me] = jnp.where(which == 0, inverse_row, term_row)

    def stat_copy(k, s):
        return remote(stats.at[s], stats.at[s], ssend.at[k], srecv.at[s], other(k))

    def tell(k, carry):
        stat_copy(k, me).start()
        return carry

    lax.fori_loop(1, count, tell, 0)

    def second_pass(j, gradient):
        span = pl.ds(aligned(j * chunk, chunk), chunk)
        block = keys[pl.ds(j * per, per)].reshape(chunk, width)
        paired = jnp.where(key_ids(j) == positive, 1.0, 0.0)
        weights = (escore[:, span] * inverse - paired).astype(BF16)
        return gradient + jnp.dot(weights, block, preferred_element_type=F32)

    gradient = lax.fori_loop(0, count // per, second_pass, jnp.zeros((rows, width), F32))

    def hear(k, carry):
        stat_copy(k, (me - k + count) % count).wait_recv()
        stat_copy(k, me).wait_send()
        return carry

    lax.fori_loop(1, count, hear, 0)
    loss_ref[0, 0] = jnp.sum(stats[:, 1, :]) / (count * rows)

    def mirror_pass(j, gradient):
        span = pl.ds(aligned(j * chunk, chunk), chunk)
        block = keys[pl.ds(j * per, per)].reshape(chunk, width)
        paired = jnp.where(key_ids(j) == positive, 1.0, 0.0)
        scale = jnp.concatenate([stats[j * per + t, 0:1, :] for t in range(per)], axis=1)
        weights = (escore[:, span] * scale - paired).astype(BF16)
        return gradient + jnp.dot(weights, block, preferred_element_type=F32)

    mirrored = lax.fori_loop(0, count // per, mirror_pass, jnp.zeros((rows, width), F32))
    sphere = (gradient + mirrored) * (sharpness / (count * rows))
    unit = unit_ref[...]
    raw_grad = (sphere - unit * jnp.sum(unit * sphere, axis=1, keepdims=True)) / length_ref[:, 0:1]
    grad_ref[part(z, c), :] = raw_grad.astype(BF16)

    def grad_copy(chip, k, q, device):
        span = part(chip, c)
        return start(remote(grad_ref.at[span], grad_ref.at[span], gsend.at[k], grecv.at[q], device))

    others = []
    for d in range(1, n):
        others.append(grad_copy(z, d, d, {"grp": ((z + d) % n) * 2 + c}))
    pairs = [grad_copy(z, n, n, {"grp": pair_g})]
    for d in range(1, n):
        others[d - 1].wait_recv()
        pairs.append(grad_copy((z - d + n) % n, n + d, n + d, {"grp": pair_g}))
    for copy in pairs:
        copy.wait_recv()
    for copy in started:
        copy.wait_send()
    store.wait()


def reduce_kernel(
    cycle, lane_count, grad_ref, second_ref, pooled_hbm, slope_hbm, hidden_hbm, out_ref,
    pooled_ref, slope_ref, hidden_ref, back_ref, second_grad, acc, sendb, recvb,
    load_sem, rs_send, rs_recv, ag_send, ag_recv,
):
    loads = [
        pltpu.make_async_copy(source, target, load_sem.at[i])
        for i, (source, target) in enumerate(
            ((slope_hbm, slope_ref), (hidden_hbm, hidden_ref), (pooled_hbm, pooled_ref))
        )
    ]
    for load in loads:
        load.start()
    b = lax.axis_index("blk")
    stages = cycle.bit_length() - 1
    bits = [(b // (1 << t)) % 2 for t in range(stages)]
    peers = [{"blk": b + (1 - 2 * bits[t]) * (1 << t)} for t in range(stages)]
    greet(peers)
    clips = slope_ref.shape[0]
    edge = second_ref.shape[1]
    fold = second_ref.shape[0] // edge
    total = out_ref.shape[0]
    size = total // lane_count
    unit = size // cycle
    top = pooled_ref.shape[1] // (lane_count * cycle)
    low = unit - top
    loads[0].wait()
    step = 128

    def back(i, carry):
        span = pl.ds(aligned(i * step, step), step)
        hidden_grad = lax.dot_general(
            grad_ref[span, :], second_ref[...], (((1,), (1,)), ((), ())),
            preferred_element_type=F32,
        )
        back_ref[span, :] = (hidden_grad * slope_ref[span, :]).astype(BF16)
        return carry

    lax.fori_loop(0, clips // step, back, 0)
    loads[1].wait()
    across = (((0,), (0,)), ((), ()))
    second_grad[...] = lax.dot_general(
        hidden_ref[...], grad_ref[...], across, preferred_element_type=F32
    )
    loads[2].wait()

    def produce(lane, away):
        t = orders[lane][0]
        side = (1 - bits[t]) if away else bits[t]
        units = cycle // 2
        wide = top * units
        column = aligned(lane * top * cycle + side * wide, 128)
        first = lax.dot_general(
            pooled_ref[:, pl.ds(column, wide)], back_ref[...], across,
            preferred_element_type=F32,
        )
        for j in range(units):
            at = aligned(lane * size + (side * units + j) * unit, 16)
            acc[pl.ds(at, top), :] = first[j * top : (j + 1) * top]
            for k in range(fold):
                row = aligned(k * edge + (lane * cycle + side * units + j) * low, 16)
                acc[pl.ds(at + top, low), k * edge : (k + 1) * edge] = second_grad[
                    pl.ds(row, low), :
                ]

    orders = [
        list(range(stages)) if lane % 2 == 0 else list(range(stages))[::-1]
        for lane in range(lane_count)
    ]
    current = [lane * size for lane in range(lane_count)]
    kept = [[None] * stages for _ in range(lane_count)]
    copies = {}
    finals = {}
    started = []

    def span(start, length):
        return pl.ds(aligned(start, 16), length)

    def offset(lane, i):
        return lane * size + size - (size >> i)

    def start_reduce(lane, i):
        t = orders[lane][i]
        length = size >> (i + 1)
        away = current[lane] + (1 - bits[t]) * length
        current[lane] = current[lane] + bits[t] * length
        kept[lane][i] = current[lane]
        buffer = pl.ds(offset(lane, i), length)
        sendb[buffer, :] = acc[span(away, length), :].astype(BF16)
        copy = remote(
            sendb.at[buffer], recvb.at[buffer], rs_send.at[lane, i], rs_recv.at[lane, i], peers[t]
        )
        copy.start()
        started.append(copy)
        copies[lane, i] = copy

    def start_gather(lane, i):
        t = orders[lane][i]
        rows = out_ref.at[span(kept[lane][i], size >> (i + 1))]
        copy = remote(rows, rows, ag_send.at[lane, i], ag_recv.at[lane, i], peers[t])
        copy.start()
        started.append(copy)
        finals[lane, i] = copy

    for lane in range(lane_count):
        produce(lane, True)
        start_reduce(lane, 0)
    for lane in range(lane_count):
        produce(lane, False)
    for i in range(stages):
        for lane in range(lane_count):
            copies[lane, i].wait_recv()
            length = size >> (i + 1)
            keep = span(kept[lane][i], length)
            summed = acc[keep, :] + recvb[pl.ds(offset(lane, i), length), :].astype(F32)
            if i + 1 < stages:
                acc[keep, :] = summed
                start_reduce(lane, i + 1)
            else:
                out_ref[keep, :] = summed.astype(BF16)
                start_gather(lane, i)
    for i in reversed(range(stages)):
        for lane in range(lane_count):
            finals[lane, i].wait_recv()
            if i:
                start_gather(lane, i - 1)
    for copy in started:
        copy.wait_send()


def tail_kernel(unit, fold, sum_ref, loss_ref, first_ref, second_ref, out_ref):
    block = sum_ref[...].astype(F32)
    low = second_ref.shape[1] // (block.shape[0] // unit)
    edge = second_ref.shape[2]
    top = unit - low
    for j in range(block.shape[0] // unit):
        first_ref[j * top : (j + 1) * top, :] = block[j * unit : j * unit + top]
        for t in range(fold):
            second_ref[t, j * low : (j + 1) * low, :] = block[
                j * unit + top : (j + 1) * unit, t * edge : (t + 1) * edge
            ]
    out_ref[0, 0] = loss_ref[0, 0]


VMEM = pl.BlockSpec(memory_space=pltpu.VMEM)
SMEM = pl.BlockSpec(memory_space=pltpu.SMEM)
ANY = pl.BlockSpec(memory_space=pl.ANY)
DMA = pltpu.SemaphoreType.DMA


def params(number, mib=None):
    return pltpu.CompilerParams(
        collective_id=number,
        has_side_effects=True,
        vmem_limit_bytes=None if mib is None else mib << 20,
    )


def shards(frames, counts, positives, w_first, w_second):
    rows, slot_count, width = frames.shape
    cycle = lax.axis_size("blk")
    group = lax.axis_size("grp")
    n = group // 2
    count = cycle * group
    units, edge = w_second.shape
    frame_mask = (jnp.arange(slot_count, dtype=jnp.int32)[None, :] < counts[:, None]).astype(BF16)
    summed = jnp.einsum("rf,rfc->rc", frame_mask, frames, preferred_element_type=F32)
    pooled = (summed / counts[:, None].astype(F32)).astype(BF16)
    pooled_all, preact, hidden, partial = pl.pallas_call(
        functools.partial(head_kernel, n),
        out_shape=(
            jax.ShapeDtypeStruct((group * rows, width), BF16),
            jax.ShapeDtypeStruct((group * rows, units), F32),
            jax.ShapeDtypeStruct((group * rows, units), BF16),
            jax.ShapeDtypeStruct((group * rows, edge), F32),
        ),
        in_specs=[VMEM, ANY, VMEM],
        out_specs=(ANY, ANY, ANY, VMEM),
        scratch_shapes=[
            pltpu.VMEM((width, units), BF16),
            pltpu.VMEM((group * rows, width), BF16),
            pltpu.VMEM((group * rows, units), F32),
            pltpu.VMEM((group * rows, units), BF16),
            DMA((2, n, 2)), DMA((2, n, 2)), DMA((2 * n, 2)), DMA((2 * n, 2)),
            DMA, DMA((3, n)),
        ],
        compiler_params=params(0),
        name="head",
    )(pooled, w_first, w_second)
    group_grad, loss, slope = pl.pallas_call(
        functools.partial(middle_kernel, cycle, n),
        out_shape=(
            jax.ShapeDtypeStruct((group * rows, edge), BF16),
            jax.ShapeDtypeStruct((1, 1), F32),
            jax.ShapeDtypeStruct((group * rows, units), F32),
        ),
        in_specs=[VMEM, VMEM, ANY],
        out_specs=(VMEM, SMEM, ANY),
        scratch_shapes=[
            pltpu.VMEM((group * rows, units), F32),
            DMA((2,)),
            pltpu.VMEM((n, rows, edge), F32),
            pltpu.VMEM((n, rows, edge), F32),
            pltpu.VMEM((n, rows, edge), F32),
            pltpu.VMEM((rows, edge), F32),
            pltpu.VMEM((rows, 128), F32),
            pltpu.VMEM((count, rows, edge), BF16),
            pltpu.VMEM((count, 8, rows), F32),
            pltpu.VMEM((rows, count * rows), F32),
            DMA((n,)), DMA((n,)), DMA((n,)), DMA((n,)),
            DMA((count,)), DMA((count,)), DMA((count,)), DMA((count,)),
            DMA((2 * n,)), DMA((2 * n,)),
        ],
        compiler_params=params(1),
        name="middle",
    )(partial, positives[None, :], preact)
    fold = units // edge
    total = width + units // fold
    lane_count = 4 if units // fold % (4 * cycle * 16) == 0 else 2
    stages = cycle.bit_length() - 1
    links = (lane_count, stages)
    summed = pl.pallas_call(
        functools.partial(reduce_kernel, cycle, lane_count),
        out_shape=jax.ShapeDtypeStruct((total, units), BF16),
        in_specs=[VMEM, VMEM, ANY, ANY, ANY],
        out_specs=VMEM,
        scratch_shapes=[
            pltpu.VMEM((group * rows, width), BF16),
            pltpu.VMEM((group * rows, units), F32),
            pltpu.VMEM((group * rows, units), BF16),
            pltpu.VMEM((group * rows, units), BF16),
            pltpu.VMEM((units, edge), F32),
            pltpu.VMEM((total, units), F32),
            pltpu.VMEM((total, units), BF16),
            pltpu.VMEM((total, units), BF16),
            DMA((3,)), DMA(links), DMA(links), DMA(links), DMA(links),
        ],
        compiler_params=params(2),
        name="reduce",
    )(group_grad, w_second, pooled_all, slope, hidden)
    unit = total // (lane_count * cycle)
    tiles = lane_count * cycle // 2
    first_out, second_out, loss = pl.pallas_call(
        functools.partial(tail_kernel, unit, fold),
        grid=(tiles,),
        out_shape=(
            jax.ShapeDtypeStruct((width, units), F32),
            jax.ShapeDtypeStruct((fold, units // fold, edge), F32),
            jax.ShapeDtypeStruct((1, 1), F32),
        ),
        in_specs=[pl.BlockSpec((2 * unit, units), lambda i: (i, 0)), SMEM],
        out_specs=(
            pl.BlockSpec((width // tiles, units), lambda i: (i, 0)),
            pl.BlockSpec((fold, units // fold // tiles, edge), lambda i: (0, i, 0)),
            SMEM,
        ),
        name="tail",
    )(summed, loss)
    return (loss.reshape(()), first_out, second_out.reshape(units, edge))


def solution(mesh):
    return jax.shard_map(
        shards,
        mesh=mesh,
        in_specs=(
            P(("blk", "grp"), None, None),
            P(("blk", "grp")),
            P(("blk", "grp")),
            P(None, "grp"),
            P("grp", None),
        ),
        out_specs=(P(), P(None, "grp"), P("grp", None)),
        check_vma=False,
    )
```

```python
import functools

import jax
import jax.numpy as jnp
from jax import lax
from jax.experimental import pallas as pl
from jax.experimental.pallas import tpu as pltpu
from jax.sharding import PartitionSpec as P

sharpness = 20.0
score_top = 20.0
MESH = pl.DeviceIdType.MESH
F32 = jnp.float32
BF16 = jnp.bfloat16


def aligned(start, step):
    return pl.multiple_of(start, step)


def remote(src, dst, send_sem, recv_sem, device):
    return pltpu.make_async_remote_copy(
        src_ref=src,
        dst_ref=dst,
        send_sem=send_sem,
        recv_sem=recv_sem,
        device_id=device,
        device_id_type=MESH,
    )


def head_phase(
    n, pooled_ref, second_ref, partial_ref, first_ref, all_ref, preact_ref, hidden_ref, load,
    line_send, line_recv, pair_send, pair_recv,
):
    rows = pooled_ref.shape[0]
    parts = line_send.shape[2]
    piece = rows // parts
    g = lax.axis_index("grp")
    z, c = g // 2, g % 2
    pair = {"grp": z * 2 + 1 - c}
    has_right, has_left = z < n - 1, z > 0
    ways = (
        ({"grp": g + 2}, has_right, lambda s: z - s, lambda s: z - 1 - s >= 0),
        ({"grp": g - 2}, has_left, lambda s: z + s, lambda s: z + 1 + s < n),
    )
    def rows_of(chip):
        return pl.ds(aligned(chip * 2 * rows, 2 * rows), 2 * rows)

    def spot(chip, q):
        return all_ref.at[pl.ds(aligned((chip * 2 + c) * rows + q * piece, piece), piece)]

    def line_copy(way, s, q, incoming=False):
        device, _, chip, _ = ways[way]
        dst = spot(chip(s + 1) if incoming else chip(s), q)
        src = pooled_ref.at[pl.ds(q * piece, piece)] if s == 0 and not incoming else dst
        return remote(src, dst, line_send.at[way, s, q], line_recv.at[way, s, q], device)

    def pair_copy(k, chip, q):
        dst = spot(chip, q)
        src = pooled_ref.at[pl.ds(q * piece, piece)] if k == 0 else dst
        return remote(src, dst, pair_send.at[k, q], pair_recv.at[k, q], pair)

    def head(k, chip):
        for q in range(parts):
            pair_copy(k, chip, q).wait_recv()
        span = rows_of(chip)
        preact = jnp.dot(all_ref[span, :], first_ref[...], preferred_element_type=F32)
        preact_ref[span, :] = preact
        hidden = jax.nn.gelu(preact).astype(BF16)
        hidden_ref[span, :] = hidden
        partial_ref[span, :] = jnp.dot(hidden, second_ref[...], preferred_element_type=F32)

    for q in range(parts):
        for way in range(2):

            @pl.when(ways[way][1])
            def _():
                line_copy(way, 0, q).start()

        pair_copy(0, z, q).start()
    all_ref[pl.ds(aligned(g * rows, rows), rows), :] = pooled_ref[...]
    load.wait()

    def key_of(way, s):
        return 1 + s if way == 0 else n + s

    for s in range(n - 1):
        for q in range(parts):
            for way in range(2):
                _, exists, chip, arrives = ways[way]

                @pl.when(arrives(s))
                def _():
                    line_copy(way, s, q, incoming=True).wait_recv()
                    if s + 1 < n - 1:

                        @pl.when(exists)
                        def _():
                            line_copy(way, s + 1, q).start()

                    pair_copy(key_of(way, s), chip(s + 1), q).start()

        if s == 0:
            head(0, z)
        else:
            for way in range(2):

                @pl.when(ways[way][3](s - 1))
                def _():
                    head(key_of(way, s - 1), ways[way][2](s))

    for way in range(2):

        @pl.when(ways[way][3](n - 2))
        def _():
            head(key_of(way, n - 2), ways[way][2](n - 1))

    for q in range(parts):
        pair_copy(0, z, q).wait_send()
        for way in range(2):
            _, exists, chip, arrives = ways[way]

            @pl.when(exists)
            def _():
                line_copy(way, 0, q).wait_send()

            for s in range(n - 1):

                @pl.when(arrives(s))
                def _():
                    pair_copy(key_of(way, s), chip(s + 1), q).wait_send()
                    if s + 1 < n - 1:

                        @pl.when(exists)
                        def _():
                            line_copy(way, s + 1, q).wait_send()


def middle_phase(
    cycle, n, part_ref, pos_ref, grad_ref, loss_ref, preact_ref,
    pbuf, acc, zbuf, unit_ref, length_ref, keys, stats, escore,
    psend, precv, zsend, zrecv, ksend, krecv, ssend, srecv, gsend, grecv,
):
    group = 2 * n
    count = cycle * group
    rows, width = unit_ref.shape
    b = lax.axis_index("blk")
    g = lax.axis_index("grp")
    z, c = g // 2, g % 2
    me = b * group + g
    pair_g = z * 2 + 1 - c

    def other(k):
        device = (me + k) % count
        return {"blk": device // group, "grp": device % group}

    started = []

    def start(copy):
        copy.start()
        started.append(copy)
        return copy

    def part(chip, core):
        return pl.ds(aligned((chip * 2 + core) * rows, rows), rows)

    order = list(range(1, n)) + [0]
    fromers = {}
    for d in order:
        fromers[d] = start(
            remote(
                part_ref.at[part((z + d) % n, 1 - c)], pbuf.at[d],
                psend.at[d], precv.at[d], {"grp": pair_g},
            )
        )
    sums = {}
    for d in order:
        fromers[d].wait_recv()
        total = part_ref[part((z + d) % n, c), :] + pbuf[d]
        acc[d] = total
        if d:
            sums[d] = start(
                remote(
                    acc.at[d], zbuf.at[d], zsend.at[d], zrecv.at[d],
                    {"grp": ((z + d) % n) * 2 + c},
                )
            )
    def slope(i, carry):
        span = pl.ds(aligned(i * rows, rows), rows)
        values = preact_ref[span, :]
        unused, backward = jax.vjp(jax.nn.gelu, values)
        preact_ref[span, :] = backward(jnp.ones_like(values))[0]
        return carry

    lax.fori_loop(0, group, slope, 0)
    raw = acc[0]
    for d in range(1, n):
        sums[d].wait_recv()
        raw = raw + zbuf[d]
    length = jnp.sqrt(jnp.sum(raw * raw, axis=1, keepdims=True) + 1e-06)
    unit = raw / length
    unit_ref[...] = unit
    length_ref[...] = jnp.broadcast_to(length, length_ref.shape)
    keys[me] = unit.astype(BF16)

    def slot(e, d, core):
        return ((b - e + cycle) % cycle * n + (z - d + n) % n) * 2 + core

    sent = [0]

    def send(s, device):
        k = sent[0]
        sent[0] += 1
        return start(remote(keys.at[s], keys.at[s], ksend.at[k], krecv.at[s], device))

    def arrive(s):
        remote(keys.at[s], keys.at[s], ksend.at[0], krecv.at[s], {"grp": pair_g}).wait_recv()

    for d in range(1, n):
        send(me, {"grp": ((z + d) % n) * 2 + c})
    for e in range(1, cycle):
        send(me, {"blk": (b + e) % cycle})
    send(me, {"grp": pair_g})
    for d in range(1, n):
        s = slot(0, d, c)
        arrive(s)
        for e in range(1, cycle):
            send(s, {"blk": (b + e) % cycle})
        send(s, {"grp": pair_g})
    lane = 128
    per = 4
    chunk = per * rows
    row_ids = me * rows + lax.broadcasted_iota(jnp.int32, (rows, 1), 0)
    eye = lax.broadcasted_iota(jnp.int32, (rows, rows), 0) == lax.broadcasted_iota(
        jnp.int32, (rows, rows), 1
    )
    positive = jnp.sum(jnp.where(eye, pos_ref[...].astype(F32), 0.0), axis=1, keepdims=True)
    positive = positive.astype(jnp.int32)
    mine = keys[me]

    def key_ids(j):
        return j * chunk + lax.broadcasted_iota(jnp.int32, (1, chunk), 1)

    def lanes(values):
        folded = values[:, :lane]
        for t in range(1, chunk // lane):
            folded = folded + values[:, t * lane : (t + 1) * lane]
        return folded

    def first_pass(j, carry):
        total, pos_score = carry
        block = keys[pl.ds(j * per, per)].reshape(chunk, width)
        scores = (
            lax.dot_general(mine, block, (((1,), (1,)), ((), ())), preferred_element_type=F32)
            * sharpness
        )
        ids = key_ids(j)
        terms = jnp.where(ids == row_ids, 0.0, jnp.exp(scores - score_top))
        escore[:, pl.ds(aligned(j * chunk, chunk), chunk)] = terms
        picked = jnp.where(ids == positive, scores, 0.0)
        return total + lanes(terms), pos_score + lanes(picked)

    zero = jnp.zeros((rows, lane), F32)
    carry = (zero, zero)
    chunks = group // per
    for e in range(cycle):
        if e == 1:
            for other_e in range(1, cycle):
                for d in range(n):
                    s = slot(other_e, d, c)
                    arrive(s)
                    send(s, {"grp": pair_g})
        for d in range(n):
            arrive(slot(e, d, 1 - c))
        base = (b - e + cycle) % cycle * chunks
        carry = lax.fori_loop(base, base + chunks, first_pass, carry)
    total, pos_score = carry
    total = jnp.sum(total, axis=1, keepdims=True)
    inverse = 1.0 / total
    term = jnp.log(total) + score_top - jnp.sum(pos_score, axis=1, keepdims=True)
    inverse_row = jnp.sum(jnp.where(eye, inverse, 0.0), axis=0, keepdims=True)
    term_row = jnp.sum(jnp.where(eye, term, 0.0), axis=0, keepdims=True)
    which = lax.broadcasted_iota(jnp.int32, (8, rows), 0)
    stats[me] = jnp.where(which == 0, inverse_row, term_row)

    def stat_copy(k, s):
        return remote(stats.at[s], stats.at[s], ssend.at[k], srecv.at[s], other(k))

    def tell(k, carry):
        stat_copy(k, me).start()
        return carry

    lax.fori_loop(1, count, tell, 0)

    def second_pass(j, gradient):
        span = pl.ds(aligned(j * chunk, chunk), chunk)
        block = keys[pl.ds(j * per, per)].reshape(chunk, width)
        paired = jnp.where(key_ids(j) == positive, 1.0, 0.0)
        weights = (escore[:, span] * inverse - paired).astype(BF16)
        return gradient + jnp.dot(weights, block, preferred_element_type=F32)

    gradient = lax.fori_loop(0, count // per, second_pass, jnp.zeros((rows, width), F32))

    def hear(k, carry):
        stat_copy(k, (me - k + count) % count).wait_recv()
        stat_copy(k, me).wait_send()
        return carry

    lax.fori_loop(1, count, hear, 0)
    loss_ref[0, 0] = jnp.sum(stats[:, 1, :]) / (count * rows)

    def mirror_pass(j, gradient):
        span = pl.ds(aligned(j * chunk, chunk), chunk)
        block = keys[pl.ds(j * per, per)].reshape(chunk, width)
        paired = jnp.where(key_ids(j) == positive, 1.0, 0.0)
        scale = jnp.concatenate([stats[j * per + t, 0:1, :] for t in range(per)], axis=1)
        weights = (escore[:, span] * scale - paired).astype(BF16)
        return gradient + jnp.dot(weights, block, preferred_element_type=F32)

    mirrored = lax.fori_loop(0, count // per, mirror_pass, jnp.zeros((rows, width), F32))
    sphere = (gradient + mirrored) * (sharpness / (count * rows))
    unit = unit_ref[...]
    raw_grad = (sphere - unit * jnp.sum(unit * sphere, axis=1, keepdims=True)) / length_ref[:, 0:1]
    grad_ref[part(z, c), :] = raw_grad.astype(BF16)

    def grad_copy(chip, k, q, device):
        span = part(chip, c)
        return start(remote(grad_ref.at[span], grad_ref.at[span], gsend.at[k], grecv.at[q], device))

    others = []
    for d in range(1, n):
        others.append(grad_copy(z, d, d, {"grp": ((z + d) % n) * 2 + c}))
    pairs = [grad_copy(z, n, n, {"grp": pair_g})]
    for d in range(1, n):
        others[d - 1].wait_recv()
        pairs.append(grad_copy((z - d + n) % n, n + d, n + d, {"grp": pair_g}))
    for copy in pairs:
        copy.wait_recv()
    for copy in started:
        copy.wait_send()


def reduce_phase(
    cycle, lane_count, grad_ref, second_ref, pooled_ref, slope_ref, hidden_ref, out_ref,
    back_ref, second_grad, acc, sendb, recvb,
    rs_send, rs_recv, ag_send, ag_recv,
):
    b = lax.axis_index("blk")
    stages = cycle.bit_length() - 1
    bits = [(b // (1 << t)) % 2 for t in range(stages)]
    peers = [{"blk": b + (1 - 2 * bits[t]) * (1 << t)} for t in range(stages)]
    clips = slope_ref.shape[0]
    edge = second_ref.shape[1]
    fold = second_ref.shape[0] // edge
    total = out_ref.shape[0]
    size = total // lane_count
    unit = size // cycle
    top = pooled_ref.shape[1] // (lane_count * cycle)
    low = unit - top
    step = 128

    def back(i, carry):
        span = pl.ds(aligned(i * step, step), step)
        hidden_grad = lax.dot_general(
            grad_ref[span, :], second_ref[...], (((1,), (1,)), ((), ())),
            preferred_element_type=F32,
        )
        back_ref[span, :] = (hidden_grad * slope_ref[span, :]).astype(BF16)
        return carry

    lax.fori_loop(0, clips // step, back, 0)
    across = (((0,), (0,)), ((), ()))
    second_grad[...] = lax.dot_general(
        hidden_ref[...], grad_ref[...], across, preferred_element_type=F32
    )

    def produce(lane, away):
        t = orders[lane][0]
        side = (1 - bits[t]) if away else bits[t]
        units = cycle // 2
        wide = top * units
        column = aligned(lane * top * cycle + side * wide, 128)
        first = lax.dot_general(
            pooled_ref[:, pl.ds(column, wide)], back_ref[...], across,
            preferred_element_type=F32,
        )
        for j in range(units):
            at = aligned(lane * size + (side * units + j) * unit, 16)
            acc[pl.ds(at, top), :] = first[j * top : (j + 1) * top]
            for k in range(fold):
                row = aligned(k * edge + (lane * cycle + side * units + j) * low, 16)
                acc[pl.ds(at + top, low), k * edge : (k + 1) * edge] = second_grad[
                    pl.ds(row, low), :
                ]

    orders = [
        list(range(stages)) if lane % 2 == 0 else list(range(stages))[::-1]
        for lane in range(lane_count)
    ]
    current = [lane * size for lane in range(lane_count)]
    kept = [[None] * stages for _ in range(lane_count)]
    copies = {}
    finals = {}
    started = []

    def span(start, length):
        return pl.ds(aligned(start, 16), length)

    def offset(lane, i):
        return lane * size + size - (size >> i)

    def start_reduce(lane, i):
        t = orders[lane][i]
        length = size >> (i + 1)
        away = current[lane] + (1 - bits[t]) * length
        current[lane] = current[lane] + bits[t] * length
        kept[lane][i] = current[lane]
        buffer = pl.ds(offset(lane, i), length)
        sendb[buffer, :] = acc[span(away, length), :].astype(BF16)
        copy = remote(
            sendb.at[buffer], recvb.at[buffer], rs_send.at[lane, i], rs_recv.at[lane, i], peers[t]
        )
        copy.start()
        started.append(copy)
        copies[lane, i] = copy

    def start_gather(lane, i):
        t = orders[lane][i]
        rows = out_ref.at[span(kept[lane][i], size >> (i + 1))]
        copy = remote(rows, rows, ag_send.at[lane, i], ag_recv.at[lane, i], peers[t])
        copy.start()
        started.append(copy)
        finals[lane, i] = copy

    for lane in range(lane_count):
        produce(lane, True)
        start_reduce(lane, 0)
    for lane in range(lane_count):
        produce(lane, False)
    for i in range(stages):
        for lane in range(lane_count):
            copies[lane, i].wait_recv()
            length = size >> (i + 1)
            keep = span(kept[lane][i], length)
            summed = acc[keep, :] + recvb[pl.ds(offset(lane, i), length), :].astype(F32)
            if i + 1 < stages:
                acc[keep, :] = summed
                start_reduce(lane, i + 1)
            else:
                out_ref[keep, :] = summed.astype(BF16)
                start_gather(lane, i)
    for i in reversed(range(stages)):
        for lane in range(lane_count):
            finals[lane, i].wait_recv()
            if i:
                start_gather(lane, i - 1)
    for copy in started:
        copy.wait_send()


def step_kernel(
    cycle, n, lane_count, pooled_ref, first_hbm, second_ref, pos_ref, out_ref, loss_ref,
    first_ref, all_ref, preact_ref, hidden_ref, partial_ref, grad_ref, load_sem, *rest,
):
    group = 2 * n
    count = cycle * group
    me = lax.axis_index("blk") * group + lax.axis_index("grp")
    load = pltpu.make_async_copy(first_hbm, first_ref, load_sem)
    load.start()
    barrier = pltpu.get_barrier_semaphore()

    def hello(k, carry):
        device = (me + k) % count
        pl.semaphore_signal(
            barrier, inc=1, device_id={"blk": device // group, "grp": device % group},
            device_id_type=MESH,
        )
        return carry

    lax.fori_loop(1, count, hello, 0)
    pl.semaphore_wait(barrier, count - 1)
    head_phase(
        n, pooled_ref, second_ref, partial_ref, first_ref, all_ref, preact_ref, hidden_ref, load,
        *rest[:4],
    )
    middle_phase(cycle, n, partial_ref, pos_ref, grad_ref, loss_ref, preact_ref, *rest[4:22])
    reduce_phase(
        cycle, lane_count, grad_ref, second_ref, all_ref, preact_ref, hidden_ref, out_ref,
        *rest[22:],
    )


def tail_kernel(unit, fold, sum_ref, loss_ref, first_ref, second_ref, out_ref):
    block = sum_ref[...].astype(F32)
    low = second_ref.shape[1] // (block.shape[0] // unit)
    edge = second_ref.shape[2]
    top = unit - low
    for j in range(block.shape[0] // unit):
        first_ref[j * top : (j + 1) * top, :] = block[j * unit : j * unit + top]
        for t in range(fold):
            second_ref[t, j * low : (j + 1) * low, :] = block[
                j * unit + top : (j + 1) * unit, t * edge : (t + 1) * edge
            ]
    out_ref[0, 0] = loss_ref[0, 0]


VMEM = pl.BlockSpec(memory_space=pltpu.VMEM)
SMEM = pl.BlockSpec(memory_space=pltpu.SMEM)
ANY = pl.BlockSpec(memory_space=pl.ANY)
DMA = pltpu.SemaphoreType.DMA


def params(number, mib=None):
    return pltpu.CompilerParams(
        collective_id=number,
        has_side_effects=True,
        vmem_limit_bytes=None if mib is None else mib << 20,
    )


def shards(frames, counts, positives, w_first, w_second):
    rows, slot_count, width = frames.shape
    cycle = lax.axis_size("blk")
    group = lax.axis_size("grp")
    n = group // 2
    count = cycle * group
    units, edge = w_second.shape
    frame_mask = (jnp.arange(slot_count, dtype=jnp.int32)[None, :] < counts[:, None]).astype(BF16)
    summed = jnp.einsum("rf,rfc->rc", frame_mask, frames, preferred_element_type=F32)
    pooled = (summed / counts[:, None].astype(F32)).astype(BF16)
    fold = units // edge
    total = width + units // fold
    lane_count = 4 if units // fold % (4 * cycle * 16) == 0 else 2
    stages = cycle.bit_length() - 1
    links = (lane_count, stages)
    summed, loss = pl.pallas_call(
        functools.partial(step_kernel, cycle, n, lane_count),
        out_shape=(
            jax.ShapeDtypeStruct((total, units), BF16),
            jax.ShapeDtypeStruct((1, 1), F32),
        ),
        in_specs=[VMEM, ANY, VMEM, VMEM],
        out_specs=(VMEM, SMEM),
        scratch_shapes=[
            pltpu.VMEM((width, units), BF16),
            pltpu.VMEM((group * rows, width), BF16),
            pltpu.VMEM((group * rows, units), F32),
            pltpu.VMEM((group * rows, units), BF16),
            pltpu.VMEM((group * rows, edge), F32),
            pltpu.VMEM((group * rows, edge), BF16),
            DMA,
            DMA((2, n, 2)), DMA((2, n, 2)), DMA((2 * n, 2)), DMA((2 * n, 2)),
            pltpu.VMEM((n, rows, edge), F32),
            pltpu.VMEM((n, rows, edge), F32),
            pltpu.VMEM((n, rows, edge), F32),
            pltpu.VMEM((rows, edge), F32),
            pltpu.VMEM((rows, 128), F32),
            pltpu.VMEM((count, rows, edge), BF16),
            pltpu.VMEM((count, 8, rows), F32),
            pltpu.VMEM((rows, count * rows), F32),
            DMA((n,)), DMA((n,)), DMA((n,)), DMA((n,)),
            DMA((count,)), DMA((count,)), DMA((count,)), DMA((count,)),
            DMA((2 * n,)), DMA((2 * n,)),
            pltpu.VMEM((group * rows, units), BF16),
            pltpu.VMEM((units, edge), F32),
            pltpu.VMEM((total, units), F32),
            pltpu.VMEM((total, units), BF16),
            pltpu.VMEM((total, units), BF16),
            DMA(links), DMA(links), DMA(links), DMA(links),
        ],
        compiler_params=params(0),
        name="step",
    )(pooled, w_first, w_second, positives[None, :])
    unit = total // (lane_count * cycle)
    tiles = lane_count * cycle // 2
    first_out, second_out, loss = pl.pallas_call(
        functools.partial(tail_kernel, unit, fold),
        grid=(tiles,),
        out_shape=(
            jax.ShapeDtypeStruct((width, units), F32),
            jax.ShapeDtypeStruct((fold, units // fold, edge), F32),
            jax.ShapeDtypeStruct((1, 1), F32),
        ),
        in_specs=[pl.BlockSpec((2 * unit, units), lambda i: (i, 0)), SMEM],
        out_specs=(
            pl.BlockSpec((width // tiles, units), lambda i: (i, 0)),
            pl.BlockSpec((fold, units // fold // tiles, edge), lambda i: (0, i, 0)),
            SMEM,
        ),
        name="tail",
    )(summed, loss)
    return (loss.reshape(()), first_out, second_out.reshape(units, edge))


def solution(mesh):
    return jax.shard_map(
        shards,
        mesh=mesh,
        in_specs=(
            P(("blk", "grp"), None, None),
            P(("blk", "grp")),
            P(("blk", "grp")),
            P(None, "grp"),
            P("grp", None),
        ),
        out_specs=(P(), P(None, "grp"), P("grp", None)),
        check_vma=False,
    )
```
